32 devices in a mesh: ens: 2 (over y), lat: 16 (over z, x, core).
Axes of the slice: x: 2, y: 2, z: 4, core: 2. Of those that a mesh axis runs over, the one named last changes fastest.
Arguments:
- field: bfloat16 [128, 1440, 384], P(('ens', 'lat')), parts along dimension 0, may hold values from -6 to 6
- norm_gain: float32 [384], replicated, may hold values from 0.1 to 1.9
- legendre_fwd: bfloat16 [256, 256, 64], P('lat'), as said below
- legendre_inv: bfloat16 [256, 256, 64], P('lat')
- degree_gain: float32 [256, 384], replicated, may hold values from 0.5 to 2
- mix_weight: bfloat16 [2, 384, 384], replicated, may hold values from -0.21875 to 0.21875
- mlp_gain: float32 [384], replicated, may hold values from 0.1 to 1.9
- up_weight: bfloat16 [384, 768], replicated, may hold values from -0.3125 to 0.3125
- up_bias: float32 [768], replicated, may hold values from -4 to 4
- down_weight: bfloat16 [768, 384], replicated, may hold values from -0.21875 to 0.21875
Outputs:
- result: bfloat16 [128, 1440, 384], P(('ens', 'lat')), parts along dimension 0
The draws below stay inside these ranges and needn't reach their ends.
There are 2 independent parts, one for each index of `ens`. The reference program is written for one: setup_inputs(seed, part) draws one part's arguments, and reference() takes and returns one part's arrays. A program takes and returns all parts, laid end to end along the dimension named above; an argument that names none is the same for every part. Nothing has to cross between parts.
Inputs may be any that keep to these rules, and one draw needn't show every extreme that they name: legendre_inv holds orthonormal associated Legendre functions of degree l and order m (zero where l < m) at the grid's colatitudes, legendre_fwd the same times each row's quadrature weight.
All inputs are finite; a program needn't handle non-finite values.
Results may differ from the reference program's by a relative error of at most 0.009.
Values may be sent and summed in bfloat16 or wider, within the bound.
A program may use at most 64 MiB of HBM per device.

```python
import math
import jax
import jax.numpy as jnp
from jax import lax

C = 384
NLON = 1440
MLP_WIDTH = 768
MMAX = 256
LAT_DEV = 4
LMAX = 256
LATITUDE_ROWS = 64
N_LAT = 16


def legendre_tables(key):
    jitter = 0.4
    shift = jax.random.uniform(jax.random.fold_in(key, 7), (LATITUDE_ROWS,), jnp.float32)
    rows = jnp.arange(LATITUDE_ROWS, dtype=jnp.int32).astype(jnp.float32)
    colatitude_angle = math.pi * (rows + 0.5 + jitter * (shift - 0.5)) / LATITUDE_ROWS
    zval = jnp.cos(colatitude_angle)[None, :]
    sine_value = jnp.sin(colatitude_angle)[None, :]
    quadrature_weight = math.pi / LATITUDE_ROWS * sine_value
    harmonic_order = jnp.arange(MMAX, dtype=jnp.int32).astype(jnp.float32)[:, None]
    ks = jnp.arange(1, MMAX, dtype=jnp.int32).astype(jnp.float32)
    partial_logs = jnp.concatenate([jnp.zeros((1,), jnp.float32), jnp.cumsum(jnp.log((2.0 * ks - 1.0) / (2.0 * ks)))])[:, None]
    log_norm_factor = 0.5 * jnp.log((2.0 * harmonic_order + 1.0) / (4.0 * math.pi)) + 0.5 * partial_logs
    diagonal_terms = jnp.exp(log_norm_factor + harmonic_order * jnp.log(sine_value))

    def step(carry, degree):
        before, last = carry
        lval = degree.astype(jnp.float32)
        alpha = jnp.sqrt((4.0 * lval * lval - 1.0) / jnp.maximum(lval * lval - harmonic_order * harmonic_order, 1.0))
        beta = jnp.sqrt(jnp.maximum((lval - 1.0) ** 2 - harmonic_order * harmonic_order, 0.0) / jnp.maximum(4.0 * (lval - 1.0) ** 2 - 1.0, 1.0))
        recur = alpha * (zval * last - beta * before)
        value = jnp.where(lval < harmonic_order, 0.0, jnp.where(lval == harmonic_order, diagonal_terms, recur))
        return ((last, value), value)
    start = jnp.zeros((MMAX, LATITUDE_ROWS), jnp.float32)
    unused, values = lax.scan(step, (start, start), jnp.arange(LMAX, dtype=jnp.int32))
    table = jnp.transpose(values, (1, 0, 2))
    return (table, table * quadrature_weight[None, :, :])


def draw_legendre_fwd(key, part):
    return legendre_tables(key)[1].astype(jnp.bfloat16)


def draw_legendre_inv(key, part):
    return legendre_tables(key)[0].astype(jnp.bfloat16)


def shard_levels(stream_key, extent, shards, low, top_value):
    factor_of = 1.0
    for axis_at, parts in shards:
        heights = jax.random.uniform(jax.random.fold_in(jax.random.fold_in(stream_key, 6), axis_at), (parts,), jnp.float32, low / len(shards), top_value / len(shards))
        factor_of = factor_of * jnp.repeat(jnp.exp(heights), extent[axis_at] // parts).reshape((-1,) + (1,) * (len(extent) - 1 - axis_at))
    return factor_of


def gaussian(rng, extent, width, most, cuts=(), kind=jnp.bfloat16):
    values = width * jax.random.normal(rng, extent, jnp.float32)
    if cuts:
        values = values * shard_levels(rng, extent, cuts, -0.22, 0.18)
    return jnp.clip(values, -most, most).astype(kind)


def setup_inputs(seed: int = 0, part: int = 0) -> dict:
    splits = jax.random.split(jax.random.key(seed), 11)
    own_keys = jax.random.split(jax.random.fold_in(splits[10], part), 11)
    field = gaussian(own_keys[0], (LATITUDE_ROWS, NLON, C), 1.0, 6.0, ((0, 16),))
    norm_gain = jnp.clip(1.0 + 0.18 * jax.random.normal(splits[1], (C,), jnp.float32), 0.1, 1.9)
    legendre_fwd = draw_legendre_fwd(jax.random.fold_in(splits[10], 71), part)
    legendre_inv = draw_legendre_inv(jax.random.fold_in(splits[10], 71), part)
    degree_gain = jnp.clip(jnp.exp(jax.random.uniform(splits[4], (LMAX, C), jnp.float32, math.log(0.5), math.log(2.0))), 0.5, 2.0)
    mix_weight = gaussian(splits[5], (2, C, C), (2 * C) ** -0.5, 0.21875)
    mlp_gain = jnp.clip(1.0 + 0.18 * jax.random.normal(splits[6], (C,), jnp.float32), 0.1, 1.9)
    up_weight = gaussian(splits[7], (C, MLP_WIDTH), C ** -0.5, 0.3125)
    up_bias = gaussian(splits[8], (MLP_WIDTH,), 0.7, 4.0, (), jnp.float32)
    down_weight = gaussian(splits[9], (MLP_WIDTH, C), MLP_WIDTH ** -0.5, 0.21875)
    return dict(field=field, norm_gain=norm_gain, legendre_fwd=legendre_fwd, legendre_inv=legendre_inv, degree_gain=degree_gain, mix_weight=mix_weight, mlp_gain=mlp_gain, up_weight=up_weight, up_bias=up_bias, down_weight=down_weight)


def dft_tables(nlon, modes):
    lon = jnp.arange(nlon, dtype=jnp.int32)
    wave = jnp.arange(modes, dtype=jnp.int32)
    phase = (wave[:, None] * lon[None, :] % nlon).astype(jnp.float32) * (2.0 * math.pi / nlon)
    scale = 2.0 * math.pi / nlon
    forward = jnp.stack([scale * jnp.cos(phase), -scale * jnp.sin(phase)], axis=1).reshape(2 * modes, nlon)
    weight = jnp.where(wave == 0, 1.0, 2.0).astype(jnp.float32)[:, None]
    inverse = jnp.stack([weight * jnp.cos(phase), -weight * jnp.sin(phase)], axis=1).reshape(2 * modes, nlon)
    return (forward.astype(jnp.bfloat16), inverse.T.astype(jnp.bfloat16))

def layer_norm(values, gain):
    values = values.astype(jnp.float32)
    center = values - lax.optimization_barrier(jnp.mean(values, axis=-1, keepdims=True))
    spread = lax.optimization_barrier(jnp.mean(center * center, axis=-1, keepdims=True))
    return center * lax.rsqrt(spread + 1e-05) * gain

def reference(field, norm_gain, legendre_fwd, legendre_inv, degree_gain, mix_weight, mlp_gain, up_weight, up_bias, down_weight):
    forward, inverse = dft_tables(NLON, MMAX)
    blocks = field.reshape(N_LAT, LAT_DEV, NLON, C)

    def analyse(block):
        normed = layer_norm(block, norm_gain).astype(jnp.bfloat16)
        spec = jnp.einsum('nk,jkc->jnc', forward.astype(jnp.float32), normed.astype(jnp.float32))
        return spec.astype(jnp.bfloat16)
    spectrum_lon = lax.map(analyse, blocks).reshape(LATITUDE_ROWS, MMAX, 2, C)
    coeffs = jnp.einsum('mlj,jmrc->mlrc', legendre_fwd.astype(jnp.float32), spectrum_lon.astype(jnp.float32))
    scaled = (coeffs * degree_gain[None, :, None, :]).astype(jnp.bfloat16).reshape(MMAX * LMAX, 2 * C)
    block_w = jnp.concatenate([jnp.concatenate([mix_weight[0], mix_weight[1]], 1), jnp.concatenate([-mix_weight[1], mix_weight[0]], 1)], 0)
    mixed = jnp.dot(scaled, block_w, preferred_element_type=jnp.float32).astype(jnp.bfloat16).reshape(MMAX, LMAX, 2, C)
    synth_lon = jnp.einsum('mlj,mlrc->jmrc', legendre_inv.astype(jnp.float32), mixed.astype(jnp.float32)).astype(jnp.bfloat16)
    synth_blocks = synth_lon.reshape(N_LAT, LAT_DEV, 2 * MMAX, C)

    def finish(pair):
        block, synth = pair
        normed = layer_norm(block, norm_gain).astype(jnp.bfloat16)
        filtered = jnp.einsum('kn,jnc->jkc', inverse.astype(jnp.float32), synth.astype(jnp.float32))
        inner = filtered + normed.astype(jnp.float32)
        post = layer_norm(inner, mlp_gain).astype(jnp.bfloat16).reshape(LAT_DEV * NLON, C)
        hidden = jax.nn.gelu(jnp.dot(post, up_weight, preferred_element_type=jnp.float32) + up_bias).astype(jnp.bfloat16)
        out = block.reshape(LAT_DEV * NLON, C).astype(jnp.float32) + jnp.dot(hidden, down_weight, preferred_element_type=jnp.float32)
        return out.astype(jnp.bfloat16).reshape(LAT_DEV, NLON, C)
    return lax.map(finish, (blocks, synth_blocks)).reshape(LATITUDE_ROWS, NLON, C)
```

```python
import functools
import math

import jax
import jax.numpy as jnp
import numpy as np
from jax import lax
from jax.experimental import pallas as pl
from jax.experimental.pallas import tpu as pltpu
from jax.sharding import PartitionSpec as P

NLON = 1440
MMAX = 256


def dft_tables(nlon, modes):
    lon = jnp.arange(nlon, dtype=jnp.int32)
    wave = jnp.arange(modes, dtype=jnp.int32)
    phase = (wave[:, None] * lon[None, :] % nlon).astype(jnp.float32) * (2.0 * math.pi / nlon)
    scale = 2.0 * math.pi / nlon
    forward = jnp.stack([scale * jnp.cos(phase), -scale * jnp.sin(phase)], axis=1).reshape(
        2 * modes, nlon
    )
    weight = jnp.where(wave == 0, 1.0, 2.0).astype(jnp.float32)[:, None]
    inverse = jnp.stack([weight * jnp.cos(phase), -weight * jnp.sin(phase)], axis=1).reshape(
        2 * modes, nlon
    )
    return (forward.astype(jnp.bfloat16), inverse.T.astype(jnp.bfloat16))


def layer_norm(values, gain):
    values = values.astype(jnp.float32)
    center = values - jnp.mean(values, axis=-1, keepdims=True)
    spread = jnp.mean(center * center, axis=-1, keepdims=True)
    return center * lax.rsqrt(spread + 1e-05) * gain


def plain_shards(
    field,
    norm_gain,
    legendre_fwd,
    legendre_inv,
    degree_gain,
    mix_weight,
    mlp_gain,
    up_weight,
    up_bias,
    down_weight,
):
    lat_rows, nlon, chan = field.shape
    modes_here, degrees, all_lats = legendre_fwd.shape
    forward, inverse = dft_tables(NLON, MMAX)
    normed = layer_norm(field, norm_gain).astype(jnp.bfloat16)
    spectrum_lon = jnp.einsum("nk,jkc->jnc", forward, normed, preferred_element_type=jnp.float32)
    spectrum_lon = spectrum_lon.astype(jnp.bfloat16).reshape(lat_rows, MMAX, 2, chan)
    arrived = lax.all_to_all(spectrum_lon, "lat", split_axis=1, concat_axis=0, tiled=True)
    coeffs = jnp.einsum("mlj,jmrc->mlrc", legendre_fwd, arrived, preferred_element_type=jnp.float32)
    scaled = (
        (coeffs * degree_gain[None, :, None, :])
        .astype(jnp.bfloat16)
        .reshape(modes_here * degrees, 2 * chan)
    )
    block_w = jnp.concatenate(
        [
            jnp.concatenate([mix_weight[0], mix_weight[1]], 1),
            jnp.concatenate([-mix_weight[1], mix_weight[0]], 1),
        ],
        0,
    )
    mixed = (
        jnp.dot(scaled, block_w, preferred_element_type=jnp.float32)
        .astype(jnp.bfloat16)
        .reshape(modes_here, degrees, 2, chan)
    )
    synth_lon = jnp.einsum(
        "mlj,mlrc->jmrc", legendre_inv, mixed, preferred_element_type=jnp.float32
    ).astype(jnp.bfloat16)
    returned = lax.all_to_all(synth_lon, "lat", split_axis=0, concat_axis=1, tiled=True)
    rows, waves, parts, width = returned.shape
    flat = returned.reshape(rows, waves * parts, width)
    filtered = jnp.einsum("kn,jnc->jkc", inverse, flat, preferred_element_type=jnp.float32)
    inner = filtered + normed.astype(jnp.float32)
    post = layer_norm(inner, mlp_gain).astype(jnp.bfloat16).reshape(lat_rows * nlon, chan)
    hidden = jax.nn.gelu(
        jnp.dot(post, up_weight, preferred_element_type=jnp.float32) + up_bias
    ).astype(jnp.bfloat16)
    output = field.reshape(lat_rows * nlon, chan).astype(jnp.float32) + jnp.dot(
        hidden, down_weight, preferred_element_type=jnp.float32
    )
    return output.astype(jnp.bfloat16).reshape(lat_rows, nlon, chan)


CHUNKS = 2
TILE = 16
BF16, F32 = jnp.bfloat16, jnp.float32


def ordered_tables(nlon, modes, owners, chunks):
    here = modes // owners
    wave = np.arange(modes).reshape(owners, chunks, here // chunks).transpose(1, 0, 2).reshape(-1)
    phase = (wave[:, None] * np.arange(nlon)[None, :] % nlon) * (2.0 * np.pi / nlon)
    table = np.stack([np.cos(phase), -np.sin(phase)], axis=1)
    weight = np.where(wave == 0, 1.0, 2.0)[:, None, None]
    forward = (table * (2.0 * np.pi / nlon)).reshape(2 * modes, nlon)
    inverse = (table * weight).reshape(2 * modes, nlon)
    return (
        jnp.asarray(forward.astype(np.float32).astype(BF16)),
        jnp.asarray(np.ascontiguousarray(inverse.T).astype(np.float32).astype(BF16)),
    )


def normalize(values, gain):
    width = values.shape[-1]
    center = values - jnp.sum(values, axis=-1, keepdims=True) * (1.0 / width)
    spread = jnp.sum(center * center, axis=-1, keepdims=True) * (1.0 / width)
    return center * lax.rsqrt(spread + 1e-05) * gain


def kernel(
    n,
    step,
    norm_gain,
    mlp_gain,
    up_bias,
    field_h,
    forward_h,
    inverse_h,
    leg_fwd_h,
    leg_inv_h,
    degree_h,
    mix_h,
    up_h,
    down_h,
    out_h,
    field,
    normed,
    result,
    forward,
    inverse,
    leg_fwd,
    leg_inv,
    degree,
    mix,
    block_w,
    up,
    down,
    swap,
    sent,
    arrived,
    by_mode,
    synth,
    back,
    flat,
    in_sem,
    row_sem,
    out_sem,
    fs_sem,
    fr_sem,
    bs_sem,
    br_sem,
):
    rows, nlon, chan = field.shape
    chunks = sent.shape[0]
    modes_here, degrees, lats = leg_fwd.shape
    per_chunk = modes_here // chunks
    groups = lats // TILE
    owners = TILE // rows
    me = lax.axis_index("lat")

    row_copies = [
        pltpu.make_async_copy(field_h.at[r], field.at[r], row_sem.at[r]) for r in range(rows)
    ]
    loads = [
        pltpu.make_async_copy(a, b, in_sem.at[i])
        for i, (a, b) in enumerate(
            [
                (forward_h, forward),
                (leg_fwd_h, leg_fwd),
                (mix_h, mix),
                (degree_h, degree),
                (leg_inv_h, leg_inv),
                (inverse_h, inverse),
                (up_h, up),
                (down_h, down),
            ]
        )
    ]
    row_copies[0].start()
    loads[0].start()
    for copy in row_copies[1:] + loads[1:]:
        copy.start()

    def peer(t):
        offset = n // 2 + ((t + 1) // 2) * (2 * (t % 2) - 1)
        return (me + offset) % n

    barrier = pltpu.get_barrier_semaphore()

    def greet(t, carry):
        pl.semaphore_signal(
            barrier, inc=1, device_id={"lat": peer(t)}, device_id_type=pl.DeviceIdType.MESH
        )
        return carry

    lax.fori_loop(0, n - 1, greet, 0)

    def exchange(source, target, send_sem, recv_sem):
        def one(t, carry):
            to = peer(t)
            pltpu.make_async_remote_copy(
                src_ref=source(to),
                dst_ref=target(me),
                send_sem=send_sem,
                recv_sem=recv_sem,
                device_id={"lat": to},
                device_id_type=pl.DeviceIdType.MESH,
            ).start()
            return carry

        lax.fori_loop(0, n - 1, one, 0)
        pltpu.make_async_copy(source(me), target(me), recv_sem).start()

    def layer(r):
        def body(t, carry):
            at = pl.ds(pl.multiple_of(t * step, TILE), step)
            values = field[r, at, :].astype(F32)
            normed[r, at, :] = normalize(values, norm_gain[...]).astype(BF16)
            return carry

        lax.fori_loop(0, nlon // step, body, 0)

    for r in range(rows):
        row_copies[r].wait()
        layer(r)
        if r == 0:
            loads[0].wait()
        spec = jnp.dot(forward[...], normed[r], preferred_element_type=F32).astype(BF16)
        spec = spec.reshape(chunks, n, TILE, chan)
        for c in range(chunks):
            sent[c, :, r] = spec[c]
        if r == 0:
            pl.semaphore_wait(barrier, n - 1)
        exchange(
            lambda d: sent.at[0, d, r], lambda s: arrived.at[0, s, r], fs_sem.at[0], fr_sem.at[0]
        )
    for c in range(1, chunks):
        exchange(lambda d: sent.at[c, d], lambda s: arrived.at[c, s], fs_sem.at[c], fr_sem.at[c])

    for copy in loads[1:]:
        copy.wait()
    block_w[:chan, :chan] = mix[0]
    block_w[:chan, chan:] = mix[1]
    block_w[chan:, :chan] = -mix[1]
    block_w[chan:, chan:] = mix[0]
    a = lax.broadcasted_iota(jnp.int32, swap.shape, 0)
    b = lax.broadcasted_iota(jnp.int32, swap.shape, 1)
    swap[...] = ((a // TILE == b % TILE) & (a % TILE == b // TILE)).astype(F32).astype(BF16)

    def give(c, r):
        exchange(
            lambda d: back.at[c, r, d],
            lambda s: flat.at[r, c, s],
            bs_sem.at[c, r],
            br_sem.at[c, r],
        )

    for c in range(chunks):
        pltpu.make_async_copy(arrived.at[c], arrived.at[c], fr_sem.at[c]).wait()
        for g in range(groups):
            block = arrived[c, g * owners : (g + 1) * owners].reshape(TILE * TILE, chan)
            turned = jnp.dot(swap[...], block, preferred_element_type=F32).astype(BF16)
            by_mode[:, g * TILE : (g + 1) * TILE, :] = turned.reshape(TILE, TILE, chan)

        def one_mode(i, carry):
            m = c * per_chunk + i
            basis = leg_fwd[m]
            parts = [
                (
                    jnp.dot(basis, by_mode[2 * i + part], preferred_element_type=F32) * degree[...]
                ).astype(BF16)
                for part in range(2)
            ]
            scaled = jnp.concatenate(parts, axis=1)
            mixed = jnp.dot(scaled, block_w[...], preferred_element_type=F32).astype(BF16)
            rows_of = lax.dot_general(
                leg_inv[m], mixed, (((0,), (0,)), ((), ())), preferred_element_type=F32
            ).astype(BF16)
            synth[2 * i] = rows_of[:, :chan]
            synth[2 * i + 1] = rows_of[:, chan:]
            return carry

        lax.fori_loop(0, per_chunk, one_mode, 0)
        for g in range(groups):
            block = synth[:, g * TILE : (g + 1) * TILE, :].reshape(TILE * TILE, chan)
            turned = jnp.dot(swap[...], block, preferred_element_type=F32).astype(BF16)
            turned = turned.reshape(owners, rows, TILE, chan)
            for r in range(rows):
                back[c, r, g * owners : (g + 1) * owners] = turned[:, r]
        if c < chunks - 1:
            for r in range(rows // 2):
                give(c, r)
    for r in range(rows):
        for c in range(chunks):
            if c == chunks - 1 or r >= rows // 2:
                give(c, r)

    for r in range(rows):
        for c in range(chunks):
            pltpu.make_async_copy(flat.at[r, c], flat.at[r, c], br_sem.at[c, r]).wait()
        waves = flat[r].reshape(chunks * n * TILE, chan)

        def finish(t, carry):
            at = pl.ds(pl.multiple_of(t * step, TILE), step)
            inner = jnp.dot(inverse[at, :], waves, preferred_element_type=F32)
            inner = inner + normed[r, at, :].astype(F32)
            post = normalize(inner, mlp_gain[...]).astype(BF16)
            hidden = jnp.dot(post, up[...], preferred_element_type=F32) + up_bias[...]
            hidden = jax.nn.gelu(hidden).astype(BF16)
            total = field[r, at, :].astype(F32) + jnp.dot(
                hidden, down[...], preferred_element_type=F32
            )
            result[r, at, :] = total.astype(BF16)
            return carry

        lax.fori_loop(0, nlon // step, finish, 0)
        pltpu.make_async_copy(result.at[r], out_h.at[r], out_sem.at[r]).start()

    for c in range(chunks):
        piece = sent.at[c, pl.ds(0, n - 1)]
        pltpu.make_async_copy(piece, piece, fs_sem.at[c]).wait()
        for r in range(rows):
            piece = back.at[c, r, pl.ds(0, n - 1)]
            pltpu.make_async_copy(piece, piece, bs_sem.at[c, r]).wait()
    for r in range(rows):
        pltpu.make_async_copy(result.at[r], out_h.at[r], out_sem.at[r]).wait()


def shards(
    n,
    field,
    norm_gain,
    legendre_fwd,
    legendre_inv,
    degree_gain,
    mix_weight,
    mlp_gain,
    up_weight,
    up_bias,
    down_weight,
):
    args = (field, norm_gain, legendre_fwd, legendre_inv, degree_gain, mix_weight)
    args = args + (mlp_gain, up_weight, up_bias, down_weight)
    rows, nlon, chan = field.shape
    modes_here, degrees, lats = legendre_fwd.shape
    width = up_weight.shape[1]
    if 2 * modes_here != CHUNKS * TILE or TILE % rows or lats % TILE:
        return plain_shards(*args)
    forward, inverse = ordered_tables(nlon, modes_here * n, n, CHUNKS)
    step = nlon // 6 if nlon % (6 * TILE) == 0 else nlon
    any_spec = pl.BlockSpec(memory_space=pl.ANY)
    vmem = pl.BlockSpec(memory_space=pltpu.VMEM)
    dma = pltpu.SemaphoreType.DMA
    return pl.pallas_call(
        functools.partial(kernel, n, step),
        out_shape=jax.ShapeDtypeStruct(field.shape, field.dtype),
        in_specs=[vmem] * 3 + [any_spec] * 9,
        out_specs=any_spec,
        scratch_shapes=[
            pltpu.VMEM((rows, nlon, chan), BF16),
            pltpu.VMEM((rows, nlon, chan), BF16),
            pltpu.VMEM((rows, nlon, chan), BF16),
            pltpu.VMEM(forward.shape, BF16),
            pltpu.VMEM(inverse.shape, BF16),
            pltpu.VMEM(legendre_fwd.shape, BF16),
            pltpu.VMEM(legendre_inv.shape, BF16),
            pltpu.VMEM(degree_gain.shape, F32),
            pltpu.VMEM(mix_weight.shape, BF16),
            pltpu.VMEM((2 * chan, 2 * chan), BF16),
            pltpu.VMEM(up_weight.shape, BF16),
            pltpu.VMEM(down_weight.shape, BF16),
            pltpu.VMEM((TILE * TILE, TILE * TILE), BF16),
            pltpu.VMEM((CHUNKS, n, rows, TILE, chan), BF16),
            pltpu.VMEM((CHUNKS, n, rows, TILE, chan), BF16),
            pltpu.VMEM((TILE, lats, chan), BF16),
            pltpu.VMEM((TILE, lats, chan), BF16),
            pltpu.VMEM((CHUNKS, rows, n, TILE, chan), BF16),
            pltpu.VMEM((rows, CHUNKS, n, TILE, chan), BF16),
            dma((8,)),
            dma((rows,)),
            dma((rows,)),
            dma((CHUNKS,)),
            dma((CHUNKS,)),
            dma((CHUNKS, rows)),
            dma((CHUNKS, rows)),
        ],
        compiler_params=pltpu.CompilerParams(
            collective_id=0, has_side_effects=True, vmem_limit_bytes=56 << 20
        ),
    )(
        norm_gain.reshape(1, chan),
        mlp_gain.reshape(1, chan),
        up_bias.reshape(1, width),
        field,
        forward,
        inverse,
        legendre_fwd,
        legendre_inv,
        degree_gain,
        mix_weight,
        up_weight,
        down_weight,
    )


def solution(mesh):
    return jax.shard_map(
        functools.partial(shards, mesh.shape["lat"]),
        mesh=mesh,
        in_specs=(
            P(("ens", "lat"), None, None),
            P(),
            P("lat", None, None),
            P("lat", None, None),
            P(),
            P(),
            P(),
            P(),
            P(),
            P(),
        ),
        out_specs=P(("ens", "lat"), None, None),
        check_vma=False,
    )
```

```python
import functools
import math

import jax
import jax.numpy as jnp
import numpy as np
from jax import lax
from jax.experimental import pallas as pl
from jax.experimental.pallas import tpu as pltpu
from jax.sharding import PartitionSpec as P

NLON = 1440
MMAX = 256


def dft_tables(nlon, modes):
    lon = jnp.arange(nlon, dtype=jnp.int32)
    wave = jnp.arange(modes, dtype=jnp.int32)
    phase = (wave[:, None] * lon[None, :] % nlon).astype(jnp.float32) * (2.0 * math.pi / nlon)
    scale = 2.0 * math.pi / nlon
    forward = jnp.stack([scale * jnp.cos(phase), -scale * jnp.sin(phase)], axis=1).reshape(
        2 * modes, nlon
    )
    weight = jnp.where(wave == 0, 1.0, 2.0).astype(jnp.float32)[:, None]
    inverse = jnp.stack([weight * jnp.cos(phase), -weight * jnp.sin(phase)], axis=1).reshape(
        2 * modes, nlon
    )
    return (forward.astype(jnp.bfloat16), inverse.T.astype(jnp.bfloat16))


def layer_norm(values, gain):
    values = values.astype(jnp.float32)
    center = values - jnp.mean(values, axis=-1, keepdims=True)
    spread = jnp.mean(center * center, axis=-1, keepdims=True)
    return center * lax.rsqrt(spread + 1e-05) * gain


def plain_shards(
    field,
    norm_gain,
    legendre_fwd,
    legendre_inv,
    degree_gain,
    mix_weight,
    mlp_gain,
    up_weight,
    up_bias,
    down_weight,
):
    lat_rows, nlon, chan = field.shape
    modes_here, degrees, all_lats = legendre_fwd.shape
    forward, inverse = dft_tables(NLON, MMAX)
    normed = layer_norm(field, norm_gain).astype(jnp.bfloat16)
    spectrum_lon = jnp.einsum("nk,jkc->jnc", forward, normed, preferred_element_type=jnp.float32)
    spectrum_lon = spectrum_lon.astype(jnp.bfloat16).reshape(lat_rows, MMAX, 2, chan)
    arrived = lax.all_to_all(spectrum_lon, "lat", split_axis=1, concat_axis=0, tiled=True)
    coeffs = jnp.einsum("mlj,jmrc->mlrc", legendre_fwd, arrived, preferred_element_type=jnp.float32)
    scaled = (
        (coeffs * degree_gain[None, :, None, :])
        .astype(jnp.bfloat16)
        .reshape(modes_here * degrees, 2 * chan)
    )
    block_w = jnp.concatenate(
        [
            jnp.concatenate([mix_weight[0], mix_weight[1]], 1),
            jnp.concatenate([-mix_weight[1], mix_weight[0]], 1),
        ],
        0,
    )
    mixed = (
        jnp.dot(scaled, block_w, preferred_element_type=jnp.float32)
        .astype(jnp.bfloat16)
        .reshape(modes_here, degrees, 2, chan)
    )
    synth_lon = jnp.einsum(
        "mlj,mlrc->jmrc", legendre_inv, mixed, preferred_element_type=jnp.float32
    ).astype(jnp.bfloat16)
    returned = lax.all_to_all(synth_lon, "lat", split_axis=0, concat_axis=1, tiled=True)
    rows, waves, parts, width = returned.shape
    flat = returned.reshape(rows, waves * parts, width)
    filtered = jnp.einsum("kn,jnc->jkc", inverse, flat, preferred_element_type=jnp.float32)
    inner = filtered + normed.astype(jnp.float32)
    post = layer_norm(inner, mlp_gain).astype(jnp.bfloat16).reshape(lat_rows * nlon, chan)
    hidden = jax.nn.gelu(
        jnp.dot(post, up_weight, preferred_element_type=jnp.float32) + up_bias
    ).astype(jnp.bfloat16)
    output = field.reshape(lat_rows * nlon, chan).astype(jnp.float32) + jnp.dot(
        hidden, down_weight, preferred_element_type=jnp.float32
    )
    return output.astype(jnp.bfloat16).reshape(lat_rows, nlon, chan)


CHUNKS = 2
GATE1 = True
GATE2 = True
OUTV = False
UNROLL_LN, UNROLL_FIN, UNROLL_MODE = 3, 6, 2
TILE = 16
BF16, F32 = jnp.bfloat16, jnp.float32


def ordered_tables(nlon, modes, owners, chunks):
    here = modes // owners
    wave = np.arange(modes).reshape(owners, chunks, here // chunks).transpose(1, 0, 2).reshape(-1)
    phase = (wave[:, None] * np.arange(nlon)[None, :] % nlon) * (2.0 * np.pi / nlon)
    table = np.stack([np.cos(phase), -np.sin(phase)], axis=1)
    weight = np.where(wave == 0, 1.0, 2.0)[:, None, None]
    forward = (table * (2.0 * np.pi / nlon)).reshape(2 * modes, nlon)
    inverse = (table * weight).reshape(2 * modes, nlon)
    return (
        jnp.asarray(forward.astype(np.float32).astype(BF16)),
        jnp.asarray(np.ascontiguousarray(inverse.T).astype(np.float32).astype(BF16)),
    )


def normalize(values, gain):
    width = values.shape[-1]
    center = values - jnp.sum(values, axis=-1, keepdims=True) * (1.0 / width)
    spread = jnp.sum(center * center, axis=-1, keepdims=True) * (1.0 / width)
    return center * lax.rsqrt(spread + 1e-05) * gain


def kernel(
    n,
    step,
    norm_gain,
    mlp_gain,
    up_bias,
    field_h,
    forward_h,
    inverse_h,
    leg_fwd_h,
    leg_inv_h,
    degree_h,
    mix_h,
    up_h,
    down_h,
    out_h,
    field,
    normed,
    result,
    forward,
    inverse,
    leg_fwd,
    leg_inv,
    degree,
    mix,
    block_w,
    up,
    down,
    swap,
    sent,
    arrived,
    by_mode,
    synth,
    back,
    flat,
    in_sem,
    row_sem,
    out_sem,
    fs_sem,
    fr_sem,
    bs_sem,
    br_sem,
):
    rows, nlon, chan = field.shape
    chunks = sent.shape[0]
    modes_here, lats, degrees = leg_fwd.shape
    per_chunk = modes_here // chunks
    groups = lats // TILE
    owners = TILE // rows
    me = lax.axis_index("lat")
    half = forward.shape[0] // chunks

    row_copies = [
        pltpu.make_async_copy(field_h.at[r], field.at[r], row_sem.at[r]) for r in range(rows)
    ]
    loads = [
        pltpu.make_async_copy(a, b, in_sem.at[i])
        for i, (a, b) in enumerate(
            [
                (forward_h.at[:half], forward.at[:half]),
                (forward_h.at[half:], forward.at[half:]),
                (leg_fwd_h, leg_fwd),
                (mix_h, mix),
                (degree_h, degree),
                (leg_inv_h, leg_inv),
                (inverse_h, inverse),
                (up_h, up),
                (down_h, down),
            ]
        )
    ]
    row_copies[0].start()
    loads[0].start()

    def peer(t):
        offset = n // 2 + ((t + 1) // 2) * (2 * (t % 2) - 1)
        return (me + offset) % n

    barrier = pltpu.get_barrier_semaphore()

    def greet(t, carry):
        pl.semaphore_signal(
            barrier, inc=1, device_id={"lat": peer(t)}, device_id_type=pl.DeviceIdType.MESH
        )
        return carry

    lax.fori_loop(0, n - 1, greet, 0)

    def exchange(source, target, send_sem, recv_sem):
        def one(t, carry):
            to = peer(t)
            pltpu.make_async_remote_copy(
                src_ref=source(to),
                dst_ref=target(me),
                send_sem=send_sem,
                recv_sem=recv_sem,
                device_id={"lat": to},
                device_id_type=pl.DeviceIdType.MESH,
            ).start()
            return carry

        lax.fori_loop(0, n - 1, one, 0)
        pltpu.make_async_copy(source(me), target(me), recv_sem).start()

    def gone(piece, sem):
        pltpu.make_async_copy(piece, piece, sem).wait()

    def layer(r):
        def body(t, carry):
            at = pl.ds(pl.multiple_of(t * step, TILE), step)
            values = field[r, at, :].astype(F32)
            normed[r, at, :] = normalize(values, norm_gain[...]).astype(BF16)
            return carry

        lax.fori_loop(0, nlon // step, body, 0, unroll=UNROLL_LN)

    def spectrum(c, r):
        spec = jnp.dot(
            forward[c * half : (c + 1) * half, :], normed[r], preferred_element_type=F32
        )
        sent[c, :, r] = spec.astype(BF16).reshape(n, TILE, chan)

    for r in range(rows):
        row_copies[r].wait()
        if r == 0:
            for copy in row_copies[1:] + loads[1:]:
                copy.start()
        layer(r)
        if r == 0:
            loads[0].wait()
        spectrum(0, r)
        if r == 0:
            pl.semaphore_wait(barrier, n - 1)
        exchange(
            lambda d: sent.at[0, d, r], lambda s: arrived.at[0, s, r], fs_sem.at[0], fr_sem.at[0]
        )
    for copy in loads[1:]:
        copy.wait()
    for c in range(1, chunks):
        for r in range(rows):
            spectrum(c, r)
        if GATE1:
            gone(sent.at[c - 1, pl.ds(0, n - 1)], fs_sem.at[c - 1])
        exchange(lambda d: sent.at[c, d], lambda s: arrived.at[c, s], fs_sem.at[c], fr_sem.at[c])

    block_w[:chan, :chan] = mix[0]
    block_w[:chan, chan:] = mix[1]
    block_w[chan:, :chan] = -mix[1]
    block_w[chan:, chan:] = mix[0]
    a = lax.broadcasted_iota(jnp.int32, swap.shape, 0)
    b = lax.broadcasted_iota(jnp.int32, swap.shape, 1)
    swap[...] = ((a // TILE == b % TILE) & (a % TILE == b // TILE)).astype(F32).astype(BF16)

    def give(c, r):
        exchange(
            lambda d: back.at[c, r, d],
            lambda s: flat.at[r, c, s],
            bs_sem.at[c, r],
            br_sem.at[c, r],
        )

    for c in range(chunks):
        pltpu.make_async_copy(arrived.at[c], arrived.at[c], fr_sem.at[c]).wait()
        for g in range(groups):
            block = arrived[c, g * owners : (g + 1) * owners].reshape(TILE * TILE, chan)
            turned = jnp.dot(swap[...], block, preferred_element_type=F32).astype(BF16)
            by_mode[:, g * TILE : (g + 1) * TILE, :] = turned.reshape(TILE, TILE, chan)

        def one_mode(i, carry):
            m = c * per_chunk + i
            both = jnp.concatenate([by_mode[2 * i], by_mode[2 * i + 1]], axis=1)
            coeffs = lax.dot_general(
                leg_fwd[m], both, (((0,), (0,)), ((), ())), preferred_element_type=F32
            )
            parts = [coeffs[:, :chan] * degree[...], coeffs[:, chan:] * degree[...]]
            scaled = jnp.concatenate(parts, axis=1).astype(BF16)
            mixed = jnp.dot(scaled, block_w[...], preferred_element_type=F32).astype(BF16)
            rows_of = jnp.dot(leg_inv[m], mixed, preferred_element_type=F32).astype(BF16)
            synth[2 * i] = rows_of[:, :chan]
            synth[2 * i + 1] = rows_of[:, chan:]
            return carry

        lax.fori_loop(0, per_chunk, one_mode, 0, unroll=UNROLL_MODE)
        for g in range(groups):
            block = synth[:, g * TILE : (g + 1) * TILE, :].reshape(TILE * TILE, chan)
            turned = jnp.dot(swap[...], block, preferred_element_type=F32).astype(BF16)
            turned = turned.reshape(owners, rows, TILE, chan)
            for r in range(rows):
                back[c, r, g * owners : (g + 1) * owners] = turned[:, r]
        if c < chunks - 1:
            if GATE2:
                gone(sent.at[c + 1, pl.ds(0, n - 1)], fs_sem.at[c + 1])
            for r in range(rows // 2):
                give(c, r)
    for r in range(rows):
        for c in range(chunks):
            if c == chunks - 1 or r >= rows // 2:
                give(c, r)

    def finish_row(r, carry):
        for c in range(chunks):
            gone(flat.at[r, c], br_sem.at[c, r])

        def finish(t, carry):
            at = pl.ds(pl.multiple_of(t * step, TILE), step)
            waves = flat[r].reshape(chunks * n * TILE, chan)
            inner = jnp.dot(inverse[at, :], waves, preferred_element_type=F32)
            inner = inner + normed[r, at, :].astype(F32)
            post = normalize(inner, mlp_gain[...]).astype(BF16)
            hidden = jnp.dot(post, up[...], preferred_element_type=F32) + up_bias[...]
            hidden = jax.nn.gelu(hidden).astype(BF16)
            total = field[r, at, :].astype(F32) + jnp.dot(
                hidden, down[...], preferred_element_type=F32
            )
            result[r, at, :] = total.astype(BF16)
            return carry

        lax.fori_loop(0, nlon // step, finish, 0, unroll=UNROLL_FIN)
        if not OUTV:
            pltpu.make_async_copy(result.at[r], out_h.at[r], out_sem.at[r]).start()
        return carry

    lax.fori_loop(0, rows, finish_row, 0)

    for c in range(chunks):
        if not (GATE1 if c < chunks - 1 else GATE2):
            gone(sent.at[c, pl.ds(0, n - 1)], fs_sem.at[c])
        for r in range(rows):
            gone(back.at[c, r, pl.ds(0, n - 1)], bs_sem.at[c, r])
    if not OUTV:
        for r in range(rows):
            pltpu.make_async_copy(result.at[r], out_h.at[r], out_sem.at[r]).wait()


def shards(
    n,
    field,
    norm_gain,
    legendre_fwd,
    legendre_inv,
    degree_gain,
    mix_weight,
    mlp_gain,
    up_weight,
    up_bias,
    down_weight,
):
    args = (field, norm_gain, legendre_fwd, legendre_inv, degree_gain, mix_weight)
    args = args + (mlp_gain, up_weight, up_bias, down_weight)
    rows, nlon, chan = field.shape
    modes_here, degrees, lats = legendre_fwd.shape
    if 2 * modes_here != CHUNKS * TILE or TILE % rows or lats % TILE:
        return plain_shards(*args)
    forward, inverse = ordered_tables(nlon, modes_here * n, n, CHUNKS)
    step = nlon // 6 if nlon % (6 * TILE) == 0 else nlon
    any_spec = pl.BlockSpec(memory_space=pl.ANY)
    vmem = pl.BlockSpec(memory_space=pltpu.VMEM)
    dma = pltpu.SemaphoreType.DMA
    return pl.pallas_call(
        functools.partial(kernel, n, step),
        out_shape=jax.ShapeDtypeStruct(field.shape, field.dtype),
        in_specs=[vmem] * 3 + [any_spec] * 9,
        out_specs=any_spec,
        scratch_shapes=[
            pltpu.VMEM((rows, nlon, chan), BF16),
            pltpu.VMEM((rows, nlon, chan), BF16),
            pltpu.VMEM((rows, nlon, chan), BF16),
            pltpu.VMEM(forward.shape, BF16),
            pltpu.VMEM(inverse.shape, BF16),
            pltpu.VMEM((modes_here, lats, degrees), BF16),
            pltpu.VMEM((modes_here, lats, degrees), BF16),
            pltpu.VMEM(degree_gain.shape, F32),
            pltpu.VMEM(mix_weight.shape, BF16),
            pltpu.VMEM((2 * chan, 2 * chan), BF16),
            pltpu.VMEM(up_weight.shape, BF16),
            pltpu.VMEM(down_weight.shape, BF16),
            pltpu.VMEM((TILE * TILE, TILE * TILE), BF16),
            pltpu.VMEM((CHUNKS, n, rows, TILE, chan), BF16),
            pltpu.VMEM((CHUNKS, n, rows, TILE, chan), BF16),
            pltpu.VMEM((TILE, lats, chan), BF16),
            pltpu.VMEM((TILE, lats, chan), BF16),
            pltpu.VMEM((CHUNKS, rows, n, TILE, chan), BF16),
            pltpu.VMEM((rows, CHUNKS, n, TILE, chan), BF16),
            dma((9,)),
            dma((rows,)),
            dma((rows,)),
            dma((CHUNKS,)),
            dma((CHUNKS,)),
            dma((CHUNKS, rows)),
            dma((CHUNKS, rows)),
        ],
        compiler_params=pltpu.CompilerParams(
            collective_id=0, has_side_effects=True, vmem_limit_bytes=56 << 20
        ),
    )(
        norm_gain,
        mlp_gain,
        up_bias,
        field,
        forward,
        inverse,
        jnp.swapaxes(legendre_fwd, 1, 2),
        jnp.swapaxes(legendre_inv, 1, 2),
        degree_gain,
        mix_weight,
        up_weight,
        down_weight,
    )


def solution(mesh):
    return jax.shard_map(
        functools.partial(shards, mesh.shape["lat"]),
        mesh=mesh,
        in_specs=(
            P(("ens", "lat"), None, None),
            P(),
            P("lat", None, None),
            P("lat", None, None),
            P(),
            P(),
            P(),
            P(),
            P(),
            P(),
        ),
        out_specs=P(("ens", "lat"), None, None),
        check_vma=False,
    )
```
